32 devices in a mesh: ctx: 4 (over z), tp: 8 (over y, x, core).
Axes of the slice: x: 2, y: 2, z: 4, core: 2. Of those that a mesh axis runs over, the one named last changes fastest.
Arguments:
- stream: bfloat16 [2048, 4096], P('ctx'), may hold values from -6 to 6
- time_previous_token: bfloat16 [4096], replicated, may hold values from -6 to 6
- channel_previous_token: bfloat16 [4096], replicated, may hold values from -15 to 15
- head_state_initial: float32 [64, 64, 64], P('tp'), may hold values from -60 to 60
- time_norm_gain: float32 [4096], replicated, may hold values from 0.5 to 1.5
- time_norm_bias: float32 [4096], replicated, may hold values from -1.2 to 1.2
- time_shift_weights: bfloat16 [6, 4096], replicated, may hold values from 0 to 1
- receptance: bfloat16 [4096, 4096], P(None, 'tp'), may hold values from -0.09375 to 0.09375
- key_projection_matrix: bfloat16 [4096, 4096], P(None, 'tp'), may hold values from -0.09375 to 0.09375
- value_projection_matrix: bfloat16 [4096, 4096], P(None, 'tp'), may hold values from -0.09375 to 0.09375
- decay_first_factor: bfloat16 [4096, 128], replicated, may hold values from -0.09375 to 0.09375
- decay_second_factor: bfloat16 [128, 4096], P(None, 'tp'), may hold values from -1 to 1
- decay_channel_base: float32 [4096], P('tp'), may hold values from -12 to -2, as said below
- rate_first_factor: bfloat16 [4096, 128], replicated, may hold values from -0.09375 to 0.09375
- rate_second_factor: bfloat16 [128, 4096], P(None, 'tp'), may hold values from -0.5 to 0.5
- rate_channel_base: float32 [4096], P('tp'), may hold values from -1.5 to 1.5
- gate_first_factor: bfloat16 [4096, 256], replicated, may hold values from -0.09375 to 0.09375
- gate_second_factor: bfloat16 [256, 4096], P(None, 'tp'), may hold values from -0.375 to 0.375
- removal_key_scale: float32 [4096], P('tp'), may hold values from 0.5 to 1.5
- key_rate_scale: float32 [4096], P('tp'), may hold values from 0.1 to 0.7
- self_lookup_coefficient: float32 [4096], P('tp'), may hold values from -1.2 to 1.2
- head_group_gain: float32 [4096], P('tp'), may hold values from 0.5 to 1.5
- head_group_bias: float32 [4096], P('tp'), may hold values from -1.2 to 1.2
- time_output_weight: bfloat16 [4096, 4096], P('tp'), may hold values from -0.09375 to 0.09375
- channel_norm_gain: float32 [4096], replicated, may hold values from 0.5 to 1.5
- channel_norm_bias: float32 [4096], replicated, may hold values from -1.2 to 1.2
- channel_shift_weight: bfloat16 [4096], replicated, may hold values from 0 to 1
- channel_key_weight: bfloat16 [4096, 8192], P(None, 'tp'), may hold values from -0.09375 to 0.09375
- channel_value_weight: bfloat16 [8192, 4096], P('tp'), may hold values from -0.0625 to 0.0625
Outputs:
- layer_out: bfloat16 [2048, 4096], P('ctx')
The draws below stay inside these ranges and needn't reach their ends.
Inputs may be any that keep to these rules, and one draw needn't show every extreme that they name: `decay_channel_base`: Channel-wise values of the decay's base.
All inputs are finite; a program needn't handle non-finite values.
Results may differ from the reference program's by a relative error of at most 0.018.
Values may be sent and summed in bfloat16 or wider, within the bound.
A program may use at most 192 MiB of HBM per device.

```python
import math
import jax
import jax.numpy as jnp
from jax import lax

EMBED_DIMENSION = 4096
LANE_SPAN = 64
HEADS = 64
FF = 8192
RW = 128
RA = 128
RG = 256
STRETCH_LENGTH = 2048
N_TP = 8


def draw_decay_channel_base(key, part):
    head_key, level_key, spread_key = jax.random.split(jax.random.fold_in(key, 11), 3)
    lane_tally = EMBED_DIMENSION // LANE_SPAN
    fast_limit = 4
    fast_heads = jax.random.randint(head_key, (lane_tally, 1), 0, 8) < fast_limit
    level = jax.random.uniform(level_key, (lane_tally, 1), jnp.float32, math.log(0.1), math.log(0.5))
    spread = jax.random.uniform(spread_key, (lane_tally, LANE_SPAN), jnp.float32, -0.7, 0.7)
    slow_value = 0.5 - math.log(STRETCH_LENGTH) + level
    fast_value = 0.5 + math.log(1.0 / 40.0) + 0.0 * level
    base_value = jnp.where(fast_heads, fast_value, slow_value) + spread
    return base_value.reshape(EMBED_DIMENSION).astype(jnp.float32)


def level_of(stream_key, dims, shards, smallest, largest):
    def one(axis_at, shards_of):
        draws = jax.random.uniform(jax.random.fold_in(jax.random.fold_in(stream_key, 6), axis_at), (shards_of,), jnp.float32, smallest / len(shards), largest / len(shards))
        return jnp.repeat(jnp.exp(draws), dims[axis_at] // shards_of).reshape((-1,) + (1,) * (len(dims) - axis_at - 1))

    gain = one(*shards[0])
    for cut in shards[1:]:
        gain = gain * one(*cut)
    return gain


def noise(key, extent, deviation, limit, pieces=(), dtype=jnp.bfloat16):
    result = jax.random.normal(key, extent, jnp.float32) * deviation
    if len(pieces) > 0:
        result = level_of(key, extent, pieces, -0.22, 0.18) * result
    return jnp.clip(result, min=-limit, max=limit).astype(dtype)


def setup_inputs(seed: int = 0) -> dict:
    key_list = jax.random.split(jax.random.key(seed), 30)
    return {
        "stream": noise(key_list[0], (STRETCH_LENGTH, EMBED_DIMENSION), 1.0, 6.0, ((0, 4),)),
        "time_previous_token": noise(key_list[1], (EMBED_DIMENSION,), 1.0, 6.0),
        "channel_previous_token": noise(key_list[2], (EMBED_DIMENSION,), 2.5, 15.0),
        "head_state_initial": noise(key_list[3], (HEADS, LANE_SPAN, LANE_SPAN), 10.0, 60.0, ((0, 8),), jnp.float32),
        "time_norm_gain": jnp.clip(1.0 + 0.1 * jax.random.normal(key_list[4], (EMBED_DIMENSION,), jnp.float32), 0.5, 1.5),
        "time_norm_bias": noise(key_list[5], (EMBED_DIMENSION,), 0.2, 1.2, (), jnp.float32),
        "time_shift_weights": jnp.clip(jax.random.uniform(key_list[6], (6, EMBED_DIMENSION), jnp.float32, 0.0, 1.0), 0.0, 1.0).astype(jnp.bfloat16),
        "receptance": noise(key_list[7], (EMBED_DIMENSION, EMBED_DIMENSION), EMBED_DIMENSION ** -0.5, 0.09375, ((1, 8),)),
        "key_projection_matrix": noise(key_list[8], (EMBED_DIMENSION, EMBED_DIMENSION), EMBED_DIMENSION ** -0.5, 0.09375, ((1, 8),)),
        "value_projection_matrix": noise(key_list[9], (EMBED_DIMENSION, EMBED_DIMENSION), EMBED_DIMENSION ** -0.5, 0.09375, ((1, 8),)),
        "decay_first_factor": noise(key_list[10], (EMBED_DIMENSION, RW), EMBED_DIMENSION ** -0.5, 0.09375),
        "decay_second_factor": noise(key_list[11], (RW, EMBED_DIMENSION), (RW // 4) ** -0.5, 1.0, ((1, 8),)),
        "decay_channel_base": draw_decay_channel_base(jax.random.fold_in(key_list[29], 71), 0),
        "rate_first_factor": noise(key_list[13], (EMBED_DIMENSION, RA), EMBED_DIMENSION ** -0.5, 0.09375),
        "rate_second_factor": noise(key_list[14], (RA, EMBED_DIMENSION), RA ** -0.5, 0.5, ((1, 8),)),
        "rate_channel_base": jnp.clip(jax.random.uniform(key_list[15], (EMBED_DIMENSION,), jnp.float32, -1.5, 1.5) * level_of(key_list[15], (EMBED_DIMENSION,), ((0, 8),), -0.4, 0.0), -1.5, 1.5),
        "gate_first_factor": noise(key_list[16], (EMBED_DIMENSION, RG), EMBED_DIMENSION ** -0.5, 0.09375),
        "gate_second_factor": noise(key_list[17], (RG, EMBED_DIMENSION), RG ** -0.5, 0.375, ((1, 8),)),
        "removal_key_scale": jnp.clip(0.5 + 1.0 * jax.random.uniform(key_list[18], (EMBED_DIMENSION,), jnp.float32) ** level_of(key_list[18], (EMBED_DIMENSION,), ((0, 8),), -0.2, 0.2), 0.5, 1.5),
        "key_rate_scale": jnp.clip(0.1 + 0.59999999 * jax.random.uniform(key_list[19], (EMBED_DIMENSION,), jnp.float32) ** level_of(key_list[19], (EMBED_DIMENSION,), ((0, 8),), -0.2, 0.2), 0.1, 0.7),
        "self_lookup_coefficient": noise(key_list[20], (EMBED_DIMENSION,), 0.2, 1.2, ((0, 8),), jnp.float32),
        "head_group_gain": jnp.clip(1.0 + 0.1 * jax.random.normal(key_list[21], (EMBED_DIMENSION,), jnp.float32), 0.5, 1.5),
        "head_group_bias": noise(key_list[22], (EMBED_DIMENSION,), 0.2, 1.2, ((0, 8),), jnp.float32),
        "time_output_weight": noise(key_list[23], (EMBED_DIMENSION, EMBED_DIMENSION), EMBED_DIMENSION ** -0.5, 0.09375, ((0, 8),)),
        "channel_norm_gain": jnp.clip(1.0 + 0.1 * jax.random.normal(key_list[24], (EMBED_DIMENSION,), jnp.float32), 0.5, 1.5),
        "channel_norm_bias": noise(key_list[25], (EMBED_DIMENSION,), 0.2, 1.2, (), jnp.float32),
        "channel_shift_weight": jnp.clip(jax.random.uniform(key_list[26], (EMBED_DIMENSION,), jnp.float32, 0.0, 1.0), 0.0, 1.0).astype(jnp.bfloat16),
        "channel_key_weight": noise(key_list[27], (EMBED_DIMENSION, FF), EMBED_DIMENSION ** -0.5, 0.09375, ((1, 8),)),
        "channel_value_weight": noise(key_list[28], (FF, EMBED_DIMENSION), FF ** -0.5, 0.0625, ((0, 8),)),
    }


def layer_norm(matrix, gain_vec, bias_vec):
    floats = matrix.astype(jnp.float32)
    average = lax.optimization_barrier(jnp.mean(floats, axis=-1, keepdims=True))
    centered = floats - average
    variance = lax.optimization_barrier(jnp.mean(centered * centered, axis=-1, keepdims=True))
    return (centered * lax.rsqrt(variance + 1e-05) * gain_vec + bias_vec).astype(jnp.bfloat16)

def mixed_input(normed, previous, weight_vec):
    current = normed.astype(jnp.float32)
    return (current + (previous.astype(jnp.float32) - current) * weight_vec.astype(jnp.float32)).astype(jnp.bfloat16)

def group_sum(left, right, groups):
    row_total = left.shape[0]
    group_width = left.shape[1] // groups
    left_groups = left.reshape(row_total, groups, group_width).transpose(1, 0, 2)
    right_groups = right.reshape(groups, group_width, right.shape[1])

    def accumulate(running, operands):
        partial_sum = jnp.dot(operands[0], operands[1], preferred_element_type=jnp.float32)
        rounded = lax.optimization_barrier(partial_sum.astype(jnp.bfloat16))
        return (running + rounded.astype(jnp.float32), None)
    start_total = jnp.zeros((row_total, right.shape[1]), jnp.float32)
    running, unused = lax.scan(accumulate, start_total, (left_groups, right_groups))
    return running

def recurrence(head_state_initial, acceptor_real, decay, norm_key, rate, lookup_corrected, payload_real):

    def advance(state, inputs):
        recept_step, decay_step, norm_step, rate_step, key_step, value_step = inputs
        removed = jnp.einsum('hij,hj->hi', state, -norm_step, precision=lax.Precision.HIGHEST)
        state = state * decay_step[:, None, :] + removed[:, :, None] * (rate_step * norm_step)[:, None, :] + value_step[:, :, None] * key_step[:, None, :]
        output = jnp.einsum('hij,hj->hi', state, recept_step, precision=lax.Precision.HIGHEST)
        return (state, output)
    final_state, outputs = lax.scan(advance, head_state_initial, (acceptor_real, decay, norm_key, rate, lookup_corrected, payload_real))
    return outputs

def reference(stream, time_previous_token, channel_previous_token, head_state_initial, time_norm_gain, time_norm_bias, time_shift_weights, receptance, key_projection_matrix, value_projection_matrix, decay_first_factor, decay_second_factor, decay_channel_base, rate_first_factor, rate_second_factor, rate_channel_base, gate_first_factor, gate_second_factor, removal_key_scale, key_rate_scale, self_lookup_coefficient, head_group_gain, head_group_bias, time_output_weight, channel_norm_gain, channel_norm_bias, channel_shift_weight, channel_key_weight, channel_value_weight):
    lane_tally = EMBED_DIMENSION // LANE_SPAN
    normed = layer_norm(stream, time_norm_gain, time_norm_bias)
    previous = jnp.concatenate([time_previous_token[None, :], normed[:-1]], axis=0)
    inputs = [mixed_input(normed, previous, time_shift_weights[position]) for position in range(6)]
    recept = jnp.dot(inputs[0], receptance, preferred_element_type=jnp.float32).astype(jnp.bfloat16)
    key_proj = jnp.dot(inputs[2], key_projection_matrix, preferred_element_type=jnp.float32).astype(jnp.bfloat16)
    value_proj = jnp.dot(inputs[3], value_projection_matrix, preferred_element_type=jnp.float32).astype(jnp.bfloat16)
    decay_low = jnp.tanh(jnp.dot(inputs[1], decay_first_factor, preferred_element_type=jnp.float32)).astype(jnp.bfloat16)
    decay_raw = decay_channel_base + jnp.dot(decay_low, decay_second_factor, preferred_element_type=jnp.float32)
    log_decay = -jnp.exp(-jax.nn.softplus(-decay_raw) - 0.5)
    decay = jnp.exp(log_decay)
    rate_low = jnp.dot(inputs[4], rate_first_factor, preferred_element_type=jnp.float32).astype(jnp.bfloat16)
    rate = jax.nn.sigmoid(rate_channel_base + jnp.dot(rate_low, rate_second_factor, preferred_element_type=jnp.float32))
    gate_low = jax.nn.sigmoid(jnp.dot(inputs[5], gate_first_factor, preferred_element_type=jnp.float32)).astype(jnp.bfloat16)
    sigmoid_valve = jnp.dot(gate_low, gate_second_factor, preferred_element_type=jnp.float32)
    shape3 = (STRETCH_LENGTH, lane_tally, LANE_SPAN)
    key_rows = key_proj.astype(jnp.float32).reshape(shape3)
    scaled = key_rows * removal_key_scale.reshape(lane_tally, LANE_SPAN)
    norm_key = scaled * lax.rsqrt(lax.optimization_barrier(jnp.sum(scaled * scaled, axis=-1, keepdims=True)) + 1e-06)
    rate_rows = rate.reshape(shape3)
    lookup_corrected = key_rows * (1.0 + (rate_rows - 1.0) * key_rate_scale.reshape(lane_tally, LANE_SPAN))
    acceptor_real = recept.astype(jnp.float32).reshape(shape3)
    payload_real = value_proj.astype(jnp.float32).reshape(shape3)
    wkv = recurrence(head_state_initial, acceptor_real, decay.reshape(shape3), norm_key, rate_rows, lookup_corrected, payload_real)
    average = lax.optimization_barrier(jnp.mean(wkv, axis=-1, keepdims=True))
    centered = wkv - average
    variance = lax.optimization_barrier(jnp.mean(centered * centered, axis=-1, keepdims=True))
    lanewise_standardized = (centered * lax.rsqrt(variance + 0.00064)).reshape(STRETCH_LENGTH, EMBED_DIMENSION) * head_group_gain + head_group_bias
    diagonal_extra = lax.optimization_barrier(jnp.sum(acceptor_real * lookup_corrected * self_lookup_coefficient.reshape(lane_tally, LANE_SPAN), axis=-1, keepdims=True)) * payload_real
    lagged_embedding = ((lanewise_standardized + diagonal_extra.reshape(STRETCH_LENGTH, EMBED_DIMENSION)) * sigmoid_valve).astype(jnp.bfloat16)
    attended = group_sum(lagged_embedding, time_output_weight, N_TP)
    middle = (stream.astype(jnp.float32) + attended).astype(jnp.bfloat16)
    normed_next = layer_norm(middle, channel_norm_gain, channel_norm_bias)
    previous_next = jnp.concatenate([channel_previous_token[None, :], normed_next[:-1]], axis=0)
    channel_in = mixed_input(normed_next, previous_next, channel_shift_weight)
    expanded = jnp.maximum(jnp.dot(channel_in, channel_key_weight, preferred_element_type=jnp.float32), 0.0)
    hidden = (expanded * expanded).astype(jnp.bfloat16)
    channel = group_sum(hidden, channel_value_weight, N_TP)
    return (middle.astype(jnp.float32) + channel).astype(jnp.bfloat16)
```

```python
import functools

import jax
import jax.numpy as jnp
from jax import lax
from jax.experimental import pallas as pl
from jax.experimental.pallas import tpu as pltpu
from jax.sharding import PartitionSpec as P

LANE_SPAN = 64
SPAN = 64
PAIR = 2 * LANE_SPAN
F32 = jnp.float32
BF16 = jnp.bfloat16


def passed_along(shard, axis, by):
    length = lax.axis_size(axis)
    pairs = [(i, i + by) for i in range(length) if 0 <= i + by < length]
    return lax.ppermute(shard, axis, pairs)


def layer_norm(matrix, gain_vec, bias_vec):
    floats = matrix.astype(jnp.float32)
    average = jnp.mean(floats, axis=-1, keepdims=True)
    centered = floats - average
    variance = jnp.mean(centered * centered, axis=-1, keepdims=True)
    return (centered * lax.rsqrt(variance + 1e-05) * gain_vec + bias_vec).astype(jnp.bfloat16)


def mixed_input(normed, previous, weight_vec):
    current = normed.astype(jnp.float32)
    return (
        current + (previous.astype(jnp.float32) - current) * weight_vec.astype(jnp.float32)
    ).astype(jnp.bfloat16)


def mm(left, right):
    return jnp.dot(left.astype(BF16), right.astype(BF16), preferred_element_type=F32)


def mm_rt(left, right):
    return lax.dot_general(
        left.astype(BF16),
        right.astype(BF16),
        (((1,), (1,)), ((), ())),
        preferred_element_type=F32,
    )


def mm_lt(left, right):
    return lax.dot_general(
        left.astype(BF16),
        right.astype(BF16),
        (((0,), (0,)), ((), ())),
        preferred_element_type=F32,
    )


def split2(matrix):
    high = matrix.astype(BF16)
    return high, (matrix - high.astype(F32)).astype(BF16)


def head_ones():
    row = lax.broadcasted_iota(jnp.int32, (PAIR, PAIR), 0)
    col = lax.broadcasted_iota(jnp.int32, (PAIR, PAIR), 1)
    return ((row < LANE_SPAN) == (col < LANE_SPAN)).astype(BF16)


def head_sum(matrix, ones):
    high, low = split2(matrix)
    return jnp.dot(high, ones, preferred_element_type=F32) + jnp.dot(
        low, ones, preferred_element_type=F32
    )


def widened(matrix, same):
    return jnp.where(same, jnp.concatenate([matrix, matrix], axis=0), 0.0)


def folded(matrix):
    return matrix[:LANE_SPAN] + matrix[LANE_SPAN:]


def local_kernel(
    recept_ref, key_ref, value_ref, dlow_ref, rlow_ref, dsec_ref, rsec_ref, vec_ref,
    zero_ref, reader_ref, extra_ref, moved_ref,
    alpha_s, beta_s, logd_s, kadj_s,
):
    spans = recept_ref.shape[0] // SPAN
    ones = head_ones()
    vec = vec_ref[...]
    decay_raw = vec[0:1] + jnp.dot(dlow_ref[...], dsec_ref[...], preferred_element_type=F32)
    soft = jnp.maximum(-decay_raw, 0.0) + jnp.log1p(jnp.exp(-jnp.abs(decay_raw)))
    logd_s[...] = -jnp.exp(-soft - 0.5)
    rate = jax.nn.sigmoid(
        vec[1:2] + jnp.dot(rlow_ref[...], rsec_ref[...], preferred_element_type=F32)
    )
    keys = key_ref[...].astype(F32)
    scaled = keys * vec[2:3]
    norm_key = scaled * lax.rsqrt(head_sum(scaled * scaled, ones) + 1e-06)
    key_adj = keys * (1.0 + (rate - 1.0) * vec[3:4])
    recept_all = recept_ref[...].astype(F32)
    extra_ref[...] = (
        head_sum(recept_all * key_adj * vec[4:5], ones) * value_ref[...].astype(F32)
    )
    alpha_s[...] = -norm_key
    beta_s[...] = rate * norm_key
    kadj_s[...] = key_adj

    row = lax.broadcasted_iota(jnp.int32, (PAIR, PAIR), 0)
    col = lax.broadcasted_iota(jnp.int32, (PAIR, PAIR), 1)
    same = (row < LANE_SPAN) == (col < LANE_SPAN)
    strict = same & (row > col)
    inclusive = same & (row >= col)
    eye = (row == col).astype(F32)
    small_row = lax.broadcasted_iota(jnp.int32, (SPAN, SPAN), 0)
    small_col = lax.broadcasted_iota(jnp.int32, (SPAN, SPAN), 1)
    lower = (small_row >= small_col).astype(BF16)

    def levels():
        size = 1
        while size < SPAN:
            yield size, (row // (2 * size) == col // (2 * size)) & (row // size > col // size)
            size *= 2

    cuts = list(levels())

    chunks = []
    for number in range(spans):
        at = pl.ds(number * SPAN, SPAN)
        logd = logd_s[at, :]
        high, low = split2(logd)
        cumulative = jnp.dot(lower, high, preferred_element_type=F32) + jnp.dot(
            lower, low, preferred_element_type=F32
        )
        before = cumulative - logd
        total = cumulative[SPAN - 1 : SPAN, :]
        centre = 0.5 * total
        alpha = alpha_s[at, :]
        beta = beta_s[at, :]
        kadj = kadj_s[at, :]
        recept = recept_ref[at, :].astype(F32)
        grow = jnp.exp(centre - cumulative)
        half = jnp.exp(centre)
        decayed = jnp.exp(before - centre)
        reading = jnp.exp(cumulative - centre)
        left = alpha * decayed
        read = recept * reading
        b_side = beta * grow
        k_side = kadj * grow
        wide_b = widened(b_side, same).astype(BF16)
        wide_k = widened(k_side, same).astype(BF16)
        wide_l = widened(left, same).astype(BF16)
        wide_r = widened(read, same).astype(BF16)
        wide_v = widened(value_ref[at, :].astype(F32), same).astype(BF16)
        pairs = mm_rt(
            jnp.concatenate([wide_l, wide_r], axis=0), jnp.concatenate([wide_b, wide_k], axis=0)
        )
        system = jnp.where(strict, pairs[:PAIR, :PAIR], 0.0)
        key_pairs = jnp.where(strict, pairs[:PAIR, PAIR:], 0.0)
        read_rate = jnp.where(inclusive, pairs[PAIR:, :PAIR], 0.0).astype(BF16)
        read_key = jnp.where(inclusive, pairs[PAIR:, PAIR:], 0.0)
        values = mm(jnp.concatenate([key_pairs, read_key], axis=0), wide_v)
        inverse = eye + jnp.where(cuts[0][1], system, 0.0)
        for size, mask in cuts[1:]:
            inverse = inverse + mm(mm(inverse, jnp.where(mask, system, 0.0)), inverse)
        right_hand = jnp.concatenate([values[:PAIR], widened(left * half, same)], axis=1)
        solved = mm(inverse, right_hand).astype(BF16)
        seen = mm(read_rate, solved)
        zero = values[PAIR:] + seen[:, :PAIR]
        reader = (widened(read * half, same) + seen[:, PAIR:]).astype(BF16)
        wide_be = widened(b_side * half, same).astype(BF16)
        wide_ke = widened(k_side * half, same).astype(BF16)
        moved = mm_lt(solved, wide_be)
        update = moved[:PAIR] + mm_lt(wide_v, wide_ke)
        chunks.append((zero, reader, moved[PAIR:].astype(BF16), update, jnp.exp(total)))

    carry = jnp.concatenate([eye, jnp.zeros((PAIR, PAIR), F32)], axis=0)
    for number, (zero, reader, change, update, fade) in enumerate(chunks):
        at = pl.ds(number * SPAN, SPAN)
        carry16 = carry.astype(BF16)
        out = mm_rt(reader, carry16)
        reader_ref[at, :] = folded(out[:, :PAIR]).astype(BF16)
        zero_ref[at, :] = folded(zero + out[:, PAIR:])
        carry = carry * fade + jnp.dot(carry16, change, preferred_element_type=F32)
        carry = jnp.concatenate([carry[:PAIR], carry[PAIR:] + update], axis=0)
    moved_ref[0, 0] = folded(carry[:PAIR]).astype(BF16)
    moved_ref[0, 1] = folded(carry[PAIR:]).astype(BF16)


def wkv_local(recept, keys, values, dlow, rlow, dsec, rsec, vec):
    tokens, width = recept.shape
    count = width // PAIR
    by_pair = pl.BlockSpec((tokens, PAIR), lambda p: (0, p))
    whole = lambda a: pl.BlockSpec(a.shape, lambda p: (0, 0))
    cols = lambda a: pl.BlockSpec((a.shape[0], PAIR), lambda p: (0, p))
    return pl.pallas_call(
        local_kernel,
        grid=(count,),
        in_specs=[by_pair, by_pair, by_pair, whole(dlow), whole(rlow), cols(dsec), cols(rsec), cols(vec)],
        out_specs=[
            by_pair,
            by_pair,
            by_pair,
            pl.BlockSpec((1, 2, LANE_SPAN, PAIR), lambda p: (p, 0, 0, 0)),
        ],
        out_shape=[
            jax.ShapeDtypeStruct((tokens, width), F32),
            jax.ShapeDtypeStruct((tokens, width), BF16),
            jax.ShapeDtypeStruct((tokens, width), F32),
            jax.ShapeDtypeStruct((count, 2, LANE_SPAN, PAIR), BF16),
        ],
        scratch_shapes=[pltpu.VMEM((tokens, PAIR), F32)] * 4,
        compiler_params=pltpu.CompilerParams(vmem_limit_bytes=48 * 1024 * 1024),
        name="wkv_local",
    )(recept, keys, values, dlow, rlow, dsec, rsec, vec)


def finish_kernel(place_ref, zero_ref, reader_ref, extra_ref, glow_ref, gsec_ref, vec_ref, state_ref, *rest):
    moved_refs, out_ref = rest[:-1], rest[-1]
    ones = head_ones()
    row = lax.broadcasted_iota(jnp.int32, (PAIR, PAIR), 0)
    col = lax.broadcasted_iota(jnp.int32, (PAIR, PAIR), 1)
    same = (row < LANE_SPAN) == (col < LANE_SPAN)
    state = jnp.concatenate([state_ref[0], state_ref[1]], axis=1)
    place = place_ref[0]
    for back in range(len(moved_refs), 0, -1):
        moved = moved_refs[back - 1]
        wide = widened(moved[0, 0].astype(F32), same).astype(BF16)
        high, low = split2(state)
        after = (
            jnp.dot(high, wide, preferred_element_type=F32)
            + jnp.dot(low, wide, preferred_element_type=F32)
            + moved[0, 1].astype(F32)
        )
        state = jnp.where(place >= back, after, state)
    wkv = zero_ref[...] + mm_rt(reader_ref[...], widened(state, same))
    scale = 1.0 / LANE_SPAN
    centered = wkv - head_sum(wkv, ones) * scale
    variance = head_sum(centered * centered, ones) * scale
    vec = vec_ref[...]
    normal = centered * lax.rsqrt(variance + 0.00064) * vec[5:6] + vec[6:7]
    gate = jnp.dot(glow_ref[...], gsec_ref[...], preferred_element_type=F32)
    out_ref[...] = ((normal + extra_ref[...]) * gate).astype(BF16)


def wkv_finish(place, zero, reader, extra, glow, gsec, vec, state, moved):
    tokens, width = zero.shape
    count = width // PAIR
    by_pair = pl.BlockSpec((tokens, PAIR), lambda p: (0, p))
    whole = lambda a: pl.BlockSpec(a.shape, lambda p: (0, 0))
    cols = lambda a: pl.BlockSpec((a.shape[0], PAIR), lambda p: (0, p))
    return pl.pallas_call(
        finish_kernel,
        grid=(count,),
        in_specs=[
            pl.BlockSpec(memory_space=pltpu.SMEM),
            by_pair,
            by_pair,
            by_pair,
            whole(glow),
            cols(gsec),
            cols(vec),
            pl.BlockSpec((2, LANE_SPAN, LANE_SPAN), lambda p: (p, 0, 0)),
        ]
        + [pl.BlockSpec((1, 2, LANE_SPAN, PAIR), lambda p: (p, 0, 0, 0))] * len(moved),
        out_specs=by_pair,
        out_shape=jax.ShapeDtypeStruct((tokens, width), BF16),
        compiler_params=pltpu.CompilerParams(vmem_limit_bytes=48 * 1024 * 1024),
        name="wkv_finish",
    )(place, zero, reader, extra, glow, gsec, vec, state, *moved)


def shards(
    stream,
    time_previous_token,
    channel_previous_token,
    head_state_initial,
    time_norm_gain,
    time_norm_bias,
    time_shift_weights,
    receptance,
    key_projection_matrix,
    value_projection_matrix,
    decay_first_factor,
    decay_second_factor,
    decay_channel_base,
    rate_first_factor,
    rate_second_factor,
    rate_channel_base,
    gate_first_factor,
    gate_second_factor,
    removal_key_scale,
    key_rate_scale,
    self_lookup_coefficient,
    head_group_gain,
    head_group_bias,
    time_output_weight,
    channel_norm_gain,
    channel_norm_bias,
    channel_shift_weight,
    channel_key_weight,
    channel_value_weight,
):
    normed = layer_norm(stream, time_norm_gain, time_norm_bias)
    ctx_place = lax.axis_index("ctx")
    ctx_first = ctx_place == 0
    arrived = passed_along(normed[-1:], "ctx", 1)
    previous = jnp.concatenate(
        [jnp.where(ctx_first, time_previous_token[None, :], arrived), normed[:-1]], axis=0
    )
    inputs = [mixed_input(normed, previous, time_shift_weights[position]) for position in range(6)]
    recept = jnp.dot(inputs[0], receptance, preferred_element_type=F32).astype(BF16)
    keys = jnp.dot(inputs[2], key_projection_matrix, preferred_element_type=F32).astype(BF16)
    values = jnp.dot(inputs[3], value_projection_matrix, preferred_element_type=F32).astype(BF16)
    decay_low = jnp.tanh(
        jnp.dot(inputs[1], decay_first_factor, preferred_element_type=F32)
    ).astype(BF16)
    rate_low = jnp.dot(inputs[4], rate_first_factor, preferred_element_type=F32).astype(BF16)
    gate_low = jax.nn.sigmoid(
        jnp.dot(inputs[5], gate_first_factor, preferred_element_type=F32)
    ).astype(BF16)
    vec = jnp.stack(
        [
            decay_channel_base,
            rate_channel_base,
            removal_key_scale,
            key_rate_scale,
            self_lookup_coefficient,
            head_group_gain,
            head_group_bias,
            head_group_bias,
        ]
    )
    zero, reader, extra, moved = wkv_local(
        recept, keys, values, decay_low, rate_low, decay_second_factor, rate_second_factor, vec
    )
    arrivals = [passed_along(moved, "ctx", by) for by in range(1, lax.axis_size("ctx"))]
    lagged_embedding = wkv_finish(
        ctx_place.reshape(1).astype(jnp.int32),
        zero,
        reader,
        extra,
        gate_low,
        gate_second_factor,
        vec,
        head_state_initial,
        arrivals,
    )
    attended = lax.psum(
        jnp.dot(lagged_embedding, time_output_weight, preferred_element_type=jnp.float32).astype(
            jnp.bfloat16
        ),
        "tp",
    ).astype(jnp.float32)
    middle = (stream.astype(jnp.float32) + attended).astype(jnp.bfloat16)
    normed_next = layer_norm(middle, channel_norm_gain, channel_norm_bias)
    arrived_next = passed_along(normed_next[-1:], "ctx", 1)
    previous_next = jnp.concatenate(
        [jnp.where(ctx_first, channel_previous_token[None, :], arrived_next), normed_next[:-1]],
        axis=0,
    )
    channel_in = mixed_input(normed_next, previous_next, channel_shift_weight)
    expanded = jnp.maximum(
        jnp.dot(channel_in, channel_key_weight, preferred_element_type=jnp.float32), 0.0
    )
    hidden = (expanded * expanded).astype(jnp.bfloat16)
    channel = lax.psum(
        jnp.dot(hidden, channel_value_weight, preferred_element_type=jnp.float32).astype(
            jnp.bfloat16
        ),
        "tp",
    ).astype(jnp.float32)
    layer_out = (middle.astype(jnp.float32) + channel).astype(jnp.bfloat16)
    return layer_out


def solution(mesh):
    placed = (
        P("ctx", None),
        P(),
        P(),
        P("tp", None, None),
        P(),
        P(),
        P(),
        P(None, "tp"),
        P(None, "tp"),
        P(None, "tp"),
        P(),
        P(None, "tp"),
        P("tp"),
        P(),
        P(None, "tp"),
        P("tp"),
        P(),
        P(None, "tp"),
        P("tp"),
        P("tp"),
        P("tp"),
        P("tp"),
        P("tp"),
        P("tp", None),
        P(),
        P(),
        P(),
        P(None, "tp"),
        P("tp", None),
    )
    return jax.shard_map(
        shards, mesh=mesh, in_specs=placed, out_specs=P("ctx", None), check_vma=False
    )
```

```python
import functools

import jax
import jax.numpy as jnp
from jax import lax
from jax.experimental import pallas as pl
from jax.experimental.pallas import tpu as pltpu
from jax.sharding import PartitionSpec as P

LANE_SPAN = 64
SPAN = 64
PAIR = 2 * LANE_SPAN
F32 = jnp.float32
BF16 = jnp.bfloat16


def passed_along(shard, axis, by):
    length = lax.axis_size(axis)
    pairs = [(i, i + by) for i in range(length) if 0 <= i + by < length]
    return lax.ppermute(shard, axis, pairs)


def layer_norm(matrix, gain_vec, bias_vec):
    floats = matrix.astype(jnp.float32)
    average = jnp.mean(floats, axis=-1, keepdims=True)
    centered = floats - average
    variance = jnp.mean(centered * centered, axis=-1, keepdims=True)
    return (centered * lax.rsqrt(variance + 1e-05) * gain_vec + bias_vec).astype(jnp.bfloat16)


def mixed_input(normed, previous, weight_vec):
    current = normed.astype(jnp.float32)
    return (
        current + (previous.astype(jnp.float32) - current) * weight_vec.astype(jnp.float32)
    ).astype(jnp.bfloat16)


def mm(left, right):
    return jnp.dot(left.astype(BF16), right.astype(BF16), preferred_element_type=F32)


def mm_rt(left, right):
    return lax.dot_general(
        left.astype(BF16),
        right.astype(BF16),
        (((1,), (1,)), ((), ())),
        preferred_element_type=F32,
    )


def mm_lt(left, right):
    return lax.dot_general(
        left.astype(BF16),
        right.astype(BF16),
        (((0,), (0,)), ((), ())),
        preferred_element_type=F32,
    )


def split2(matrix):
    high = matrix.astype(BF16)
    return high, (matrix - high.astype(F32)).astype(BF16)


def head_ones():
    row = lax.broadcasted_iota(jnp.int32, (PAIR, PAIR), 0)
    col = lax.broadcasted_iota(jnp.int32, (PAIR, PAIR), 1)
    return ((row < LANE_SPAN) == (col < LANE_SPAN)).astype(BF16)


def head_sum(matrix, ones):
    high, low = split2(matrix)
    return jnp.dot(high, ones, preferred_element_type=F32) + jnp.dot(
        low, ones, preferred_element_type=F32
    )


def widened(matrix, same):
    return jnp.where(same, jnp.concatenate([matrix, matrix], axis=0), 0.0)


def folded(matrix):
    return matrix[:LANE_SPAN] + matrix[LANE_SPAN:]


def local_kernel(
    recept_ref, key_ref, value_ref, dlow_ref, rlow_ref, dsec_ref, rsec_ref, vec_ref,
    zero_ref, reader_ref, extra_ref, moved_ref,
    alpha_s, beta_s, logd_s, kadj_s,
):
    spans = recept_ref.shape[0] // SPAN
    ones = head_ones()
    vec = vec_ref[...]
    decay_raw = vec[0:1] + jnp.dot(dlow_ref[...], dsec_ref[...], preferred_element_type=F32)
    soft = jnp.maximum(-decay_raw, 0.0) + jnp.log1p(jnp.exp(-jnp.abs(decay_raw)))
    logd_s[...] = -jnp.exp(-soft - 0.5)
    rate = jax.nn.sigmoid(
        vec[1:2] + jnp.dot(rlow_ref[...], rsec_ref[...], preferred_element_type=F32)
    )
    keys = key_ref[...].astype(F32)
    scaled = keys * vec[2:3]
    norm_key = scaled * lax.rsqrt(head_sum(scaled * scaled, ones) + 1e-06)
    key_adj = keys * (1.0 + (rate - 1.0) * vec[3:4])
    recept_all = recept_ref[...].astype(F32)
    extra_ref[...] = (
        head_sum(recept_all * key_adj * vec[4:5], ones) * value_ref[...].astype(F32)
    )
    alpha_s[...] = -norm_key
    beta_s[...] = rate * norm_key
    kadj_s[...] = key_adj

    row = lax.broadcasted_iota(jnp.int32, (PAIR, PAIR), 0)
    col = lax.broadcasted_iota(jnp.int32, (PAIR, PAIR), 1)
    same = (row < LANE_SPAN) == (col < LANE_SPAN)
    strict = same & (row > col)
    inclusive = same & (row >= col)
    eye = (row == col).astype(F32)
    small_row = lax.broadcasted_iota(jnp.int32, (SPAN, SPAN), 0)
    small_col = lax.broadcasted_iota(jnp.int32, (SPAN, SPAN), 1)
    lower = (small_row >= small_col).astype(BF16)

    def levels():
        size = 1
        while size < SPAN:
            yield size, (row // (2 * size) == col // (2 * size)) & (row // size > col // size)
            size *= 2

    cuts = list(levels())

    stage = []
    for number in range(spans):
        at = pl.ds(number * SPAN, SPAN)
        logd = logd_s[at, :]
        high, low = split2(logd)
        cumulative = jnp.dot(lower, high, preferred_element_type=F32) + jnp.dot(
            lower, low, preferred_element_type=F32
        )
        before = cumulative - logd
        total = cumulative[SPAN - 1 : SPAN, :]
        centre = 0.5 * total
        grow = jnp.exp(centre - cumulative)
        half = jnp.exp(centre)
        left = alpha_s[at, :] * jnp.exp(before - centre)
        read = recept_ref[at, :].astype(F32) * jnp.exp(cumulative - centre)
        b_side = beta_s[at, :] * grow
        k_side = kadj_s[at, :] * grow
        wide_b = widened(b_side, same).astype(BF16)
        wide_k = widened(k_side, same).astype(BF16)
        wide_l = widened(left, same).astype(BF16)
        wide_r = widened(read, same).astype(BF16)
        pairs = mm_rt(
            jnp.concatenate([wide_l, wide_r], axis=0), jnp.concatenate([wide_b, wide_k], axis=0)
        )
        system = jnp.where(strict, pairs[:PAIR, :PAIR], 0.0)
        both = jnp.concatenate(
            [
                jnp.where(strict, pairs[:PAIR, PAIR:], 0.0),
                jnp.where(inclusive, pairs[PAIR:, PAIR:], 0.0),
            ],
            axis=0,
        ).astype(BF16)
        read_rate = jnp.where(inclusive, pairs[PAIR:, :PAIR], 0.0).astype(BF16)
        stage.append(
            dict(
                at=at, half=half, total=total, system=system.astype(BF16), both=both,
                read_rate=read_rate, left=left, read=read, b_side=b_side, k_side=k_side,
                inverse=eye + jnp.where(cuts[0][1], system, 0.0),
            )
        )
    for item in stage:
        item["wide_v"] = widened(value_ref[item["at"], :].astype(F32), same).astype(BF16)
        item["values"] = mm(item["both"], item["wide_v"])
    zero16 = jnp.zeros((PAIR, PAIR), BF16)
    for size, mask in cuts[1:]:
        for item in stage:
            item["inv16"] = item["inverse"].astype(BF16)
            item["step"] = mm(item["inv16"], jnp.where(mask, item["system"], zero16)).astype(BF16)
        for item in stage:
            item["inverse"] = item["inverse"] + mm(item["step"], item["inv16"])
    for item in stage:
        right_hand = jnp.concatenate(
            [item["values"][:PAIR], widened(item["left"] * item["half"], same)], axis=1
        )
        item["solved"] = mm(item["inverse"], right_hand).astype(BF16)
    chunks = []
    for item in stage:
        half = item["half"]
        seen = mm(item["read_rate"], item["solved"])
        zero = item["values"][PAIR:] + seen[:, :PAIR]
        reader = (widened(item["read"] * half, same) + seen[:, PAIR:]).astype(BF16)
        wide_be = widened(item["b_side"] * half, same).astype(BF16)
        wide_ke = widened(item["k_side"] * half, same).astype(BF16)
        moved = mm_lt(item["solved"], wide_be)
        update = moved[:PAIR] + mm_lt(item["wide_v"], wide_ke)
        chunks.append((zero, reader, moved[PAIR:].astype(BF16), update, jnp.exp(item["total"])))

    carry = jnp.concatenate([eye, jnp.zeros((PAIR, PAIR), F32)], axis=0)
    for number, (zero, reader, change, update, fade) in enumerate(chunks):
        at = pl.ds(number * SPAN, SPAN)
        carry16 = carry.astype(BF16)
        out = mm_rt(reader, carry16)
        reader_ref[at, :] = folded(out[:, :PAIR]).astype(BF16)
        zero_ref[at, :] = folded(zero + out[:, PAIR:])
        carry = carry * fade + jnp.dot(carry16, change, preferred_element_type=F32)
        carry = jnp.concatenate([carry[:PAIR], carry[PAIR:] + update], axis=0)
    moved_ref[0, 0] = folded(carry[:PAIR]).astype(BF16)
    moved_ref[0, 1] = folded(carry[PAIR:]).astype(BF16)


def wkv_local(recept, keys, values, dlow, rlow, dsec, rsec, vec):
    tokens, width = recept.shape
    count = width // PAIR
    by_pair = pl.BlockSpec((tokens, PAIR), lambda p: (0, p))
    whole = lambda a: pl.BlockSpec(a.shape, lambda p: (0, 0))
    cols = lambda a: pl.BlockSpec((a.shape[0], PAIR), lambda p: (0, p))
    return pl.pallas_call(
        local_kernel,
        grid=(count,),
        in_specs=[by_pair, by_pair, by_pair, whole(dlow), whole(rlow), cols(dsec), cols(rsec), cols(vec)],
        out_specs=[
            by_pair,
            by_pair,
            by_pair,
            pl.BlockSpec((1, 2, LANE_SPAN, PAIR), lambda p: (p, 0, 0, 0)),
        ],
        out_shape=[
            jax.ShapeDtypeStruct((tokens, width), F32),
            jax.ShapeDtypeStruct((tokens, width), BF16),
            jax.ShapeDtypeStruct((tokens, width), F32),
            jax.ShapeDtypeStruct((count, 2, LANE_SPAN, PAIR), BF16),
        ],
        scratch_shapes=[pltpu.VMEM((tokens, PAIR), F32)] * 4,
        compiler_params=pltpu.CompilerParams(vmem_limit_bytes=48 * 1024 * 1024),
        name="wkv_local",
    )(recept, keys, values, dlow, rlow, dsec, rsec, vec)


def finish_kernel(place_ref, zero_ref, reader_ref, extra_ref, glow_ref, gsec_ref, vec_ref, state_ref, *rest):
    moved_refs, out_ref = rest[:-1], rest[-1]
    ones = head_ones()
    row = lax.broadcasted_iota(jnp.int32, (PAIR, PAIR), 0)
    col = lax.broadcasted_iota(jnp.int32, (PAIR, PAIR), 1)
    same = (row < LANE_SPAN) == (col < LANE_SPAN)
    state = jnp.concatenate([state_ref[0], state_ref[1]], axis=1)
    place = place_ref[0]
    for back in range(len(moved_refs), 0, -1):
        moved = moved_refs[back - 1]
        wide = widened(moved[0, 0].astype(F32), same).astype(BF16)
        high, low = split2(state)
        after = (
            jnp.dot(high, wide, preferred_element_type=F32)
            + jnp.dot(low, wide, preferred_element_type=F32)
            + moved[0, 1].astype(F32)
        )
        state = jnp.where(place >= back, after, state)
    wkv = zero_ref[...] + mm_rt(reader_ref[...], widened(state, same))
    scale = 1.0 / LANE_SPAN
    centered = wkv - head_sum(wkv, ones) * scale
    variance = head_sum(centered * centered, ones) * scale
    vec = vec_ref[...]
    normal = centered * lax.rsqrt(variance + 0.00064) * vec[5:6] + vec[6:7]
    gate = jnp.dot(glow_ref[...], gsec_ref[...], preferred_element_type=F32)
    out_ref[...] = ((normal + extra_ref[...]) * gate).astype(BF16)


def wkv_finish(place, zero, reader, extra, glow, gsec, vec, state, moved):
    tokens, width = zero.shape
    count = width // PAIR
    by_pair = pl.BlockSpec((tokens, PAIR), lambda p: (0, p))
    whole = lambda a: pl.BlockSpec(a.shape, lambda p: (0, 0))
    cols = lambda a: pl.BlockSpec((a.shape[0], PAIR), lambda p: (0, p))
    return pl.pallas_call(
        finish_kernel,
        grid=(count,),
        in_specs=[
            pl.BlockSpec(memory_space=pltpu.SMEM),
            by_pair,
            by_pair,
            by_pair,
            whole(glow),
            cols(gsec),
            cols(vec),
            pl.BlockSpec((2, LANE_SPAN, LANE_SPAN), lambda p: (p, 0, 0)),
        ]
        + [pl.BlockSpec((1, 2, LANE_SPAN, PAIR), lambda p: (p, 0, 0, 0))] * len(moved),
        out_specs=by_pair,
        out_shape=jax.ShapeDtypeStruct((tokens, width), BF16),
        compiler_params=pltpu.CompilerParams(vmem_limit_bytes=48 * 1024 * 1024),
        name="wkv_finish",
    )(place, zero, reader, extra, glow, gsec, vec, state, *moved)


MESH = pl.DeviceIdType.MESH


def summed_kernel(
    way, places, left_ref, right_ref, rest_ref, gain_ref, bias_ref,
    out_ref, kept_ref, part_ref, acc_ref, recv_ref,
    rs_send, rs_recv, ag_send, ag_recv,
):
    bits = places.bit_length() - 1
    tokens, width = out_ref.shape
    rows = tokens // places
    wide = width // 2
    me = lax.axis_index("tp")
    mine = [(me // (1 << d)) % 2 for d in range(bits)]
    partners = [me + (1 << d) * (1 - 2 * mine[d]) for d in range(bits)]
    orders = [list(range(bits)), list(range(1)) + list(range(bits - 1, 0, -1))]
    weight = [1 << (bits - 1 - d) for d in range(bits)]

    def frees(order, step):
        dims = order[step + 1 :]
        for code in range(1 << len(dims)):
            yield code, {d: (code >> n) % 2 for n, d in enumerate(dims)}

    def block(free, flipped=None):
        total = 0
        for d in range(bits):
            value = free[d] if d in free else (1 - mine[d] if d == flipped else mine[d])
            total = total + value * weight[d]
        return total

    def area(at, side):
        return pl.ds(pl.multiple_of(at * rows, rows), rows), pl.ds(side * wide, wide)

    barrier = pltpu.get_barrier_semaphore()
    for partner in partners:
        pl.semaphore_signal(barrier, inc=1, device_id={"tp": partner}, device_id_type=MESH)
    pl.semaphore_wait(barrier, bits)

    def product(first, side):
        group = pl.ds(pl.multiple_of(first * (tokens // 2), tokens // 2), tokens // 2)
        tile = 512

        def one(n, _):
            cols = pl.ds(pl.multiple_of(side * wide + n * tile, tile), tile)
            part_ref[group, cols] = jnp.dot(
                left_ref[group, :], right_ref[:, cols], preferred_element_type=F32
            ).astype(BF16)
            return 0

        lax.fori_loop(0, wide // tile, one, 0)

    starts = [places - (1 << (bits - step)) for step in range(bits)]
    sent = []

    def scatter(side, step, code, free):
        order = orders[side]
        dim = order[step]
        slot = starts[step] + code
        at = block(free, dim)
        source = part_ref.at[area(at, side)] if step == 0 else acc_ref.at[side, at]
        copy = pltpu.make_async_remote_copy(
            src_ref=source,
            dst_ref=recv_ref.at[side, slot],
            send_sem=rs_send.at[side, slot],
            recv_sem=rs_recv.at[side, slot],
            device_id={"tp": partners[dim]},
            device_id_type=MESH,
        )
        copy.start()
        sent.append(copy)

    def gathered(side, step, code, free):
        order = orders[side]
        slot = starts[step] + code
        at = block(free)
        pltpu.make_async_remote_copy(
            src_ref=recv_ref.at[side, slot],
            dst_ref=recv_ref.at[side, slot],
            send_sem=rs_send.at[side, slot],
            recv_sem=rs_recv.at[side, slot],
            device_id={"tp": partners[order[step]]},
            device_id_type=MESH,
        ).wait_recv()
        base = pl.multiple_of(at * rows, rows)
        tile = 16

        def one(n, _):
            here = pl.ds(pl.multiple_of(n * tile, tile), tile)
            if step == 0:
                there = pl.ds(pl.multiple_of(base + n * tile, tile), tile)
                own = part_ref[there, pl.ds(side * wide, wide)]
            else:
                own = acc_ref[side, at, here, :]
            acc_ref[side, at, here, :] = (
                own.astype(F32) + recv_ref[side, slot, here, :].astype(F32)
            ).astype(BF16)
            return 0

        lax.fori_loop(0, rows // tile, one, 0)

    for side in range(2):
        product(1 - mine[0], side)
        for code, free in frees(orders[side], 0):
            scatter(side, 0, code, free)
    for side in range(2):
        product(mine[0], side)
    for step in range(bits):
        for side in range(2):
            for code, free in frees(orders[side], step):
                gathered(side, step, code, free)
            if step + 1 < bits:
                for code, free in frees(orders[side], step + 1):
                    scatter(side, step + 1, code, free)

    here_block = block({})
    base = pl.multiple_of(here_block * rows, rows)
    tile = 16

    def finish(n, _):
        here = pl.ds(pl.multiple_of(n * tile, tile), tile)
        there = pl.ds(pl.multiple_of(base + n * tile, tile), tile)
        total = jnp.concatenate(
            [acc_ref[0, here_block, here, :], acc_ref[1, here_block, here, :]], axis=1
        ).astype(F32)
        middle = (rest_ref[here, :].astype(F32) + total).astype(BF16)
        if way == "norm":
            kept_ref[here, :] = middle
            floats = middle.astype(F32)
            centered = floats - jnp.mean(floats, axis=-1, keepdims=True)
            variance = jnp.mean(centered * centered, axis=-1, keepdims=True)
            middle = (
                centered * lax.rsqrt(variance + 1e-05) * gain_ref[...] + bias_ref[...]
            ).astype(BF16)
        out_ref[there, :] = middle
        return 0

    lax.fori_loop(0, rows // tile, finish, 0)
    if way != "norm":
        kept_ref[...] = jnp.zeros_like(kept_ref)

    def share(side, step, at):
        dim = orders[side][step]
        copy = pltpu.make_async_remote_copy(
            src_ref=out_ref.at[area(at, side)],
            dst_ref=out_ref.at[area(at, side)],
            send_sem=ag_send.at[side, step, at],
            recv_sem=ag_recv.at[side, at],
            device_id={"tp": partners[dim]},
            device_id_type=MESH,
        )
        copy.start()
        sent.append(copy)

    for step in range(bits - 1, -1, -1):
        for side in range(2):
            share(side, step, here_block)
    for step in range(bits - 1, -1, -1):
        for side in range(2):
            for code, free in frees(orders[side], step):
                at = block(free, orders[side][step])
                pltpu.make_async_remote_copy(
                    src_ref=out_ref.at[area(at, side)],
                    dst_ref=out_ref.at[area(at, side)],
                    send_sem=ag_send.at[side, step, at],
                    recv_sem=ag_recv.at[side, at],
                    device_id={"tp": partners[orders[side][step]]},
                    device_id_type=MESH,
                ).wait_recv()
                for later in range(step - 1, -1, -1):
                    share(side, later, at)
    for copy in sent:
        copy.wait_send()


def summed(way, number, left, right, rest, gain, bias):
    places = lax.axis_size("tp")
    bits = places.bit_length() - 1
    tokens = left.shape[0]
    width = right.shape[1]
    rows = tokens // places
    small = (rows, width) if way == "norm" else (8, 128)
    vmem = pl.BlockSpec(memory_space=pltpu.VMEM)
    return pl.pallas_call(
        functools.partial(summed_kernel, way, places),
        in_specs=[vmem] * 5,
        out_specs=[vmem, vmem],
        out_shape=[
            jax.ShapeDtypeStruct((tokens, width), BF16),
            jax.ShapeDtypeStruct(small, BF16),
        ],
        scratch_shapes=[
            pltpu.VMEM((tokens, width), BF16),
            pltpu.VMEM((2, places, rows, width // 2), BF16),
            pltpu.VMEM((2, places - 1, rows, width // 2), BF16),
            pltpu.SemaphoreType.DMA((2, places - 1)),
            pltpu.SemaphoreType.DMA((2, places - 1)),
            pltpu.SemaphoreType.DMA((2, bits, places)),
            pltpu.SemaphoreType.DMA((2, places)),
        ],
        compiler_params=pltpu.CompilerParams(
            collective_id=number, has_side_effects=True, vmem_limit_bytes=56 * 1024 * 1024
        ),
        name="summed_" + way,
    )(left, right, rest, gain.reshape(1, -1), bias.reshape(1, -1))


def own_rows(matrix):
    places = lax.axis_size("tp")
    bits = places.bit_length() - 1
    me = lax.axis_index("tp")
    place = sum(((me // (1 << d)) % 2) * (1 << (bits - 1 - d)) for d in range(bits))
    rows = matrix.shape[0] // places
    return lax.dynamic_slice_in_dim(matrix, place * rows, rows, axis=0)


def shards(
    stream,
    time_previous_token,
    channel_previous_token,
    head_state_initial,
    time_norm_gain,
    time_norm_bias,
    time_shift_weights,
    receptance,
    key_projection_matrix,
    value_projection_matrix,
    decay_first_factor,
    decay_second_factor,
    decay_channel_base,
    rate_first_factor,
    rate_second_factor,
    rate_channel_base,
    gate_first_factor,
    gate_second_factor,
    removal_key_scale,
    key_rate_scale,
    self_lookup_coefficient,
    head_group_gain,
    head_group_bias,
    time_output_weight,
    channel_norm_gain,
    channel_norm_bias,
    channel_shift_weight,
    channel_key_weight,
    channel_value_weight,
):
    normed = layer_norm(stream, time_norm_gain, time_norm_bias)
    ctx_place = lax.axis_index("ctx")
    ctx_first = ctx_place == 0
    arrived = passed_along(normed[-1:], "ctx", 1)
    previous = jnp.concatenate(
        [jnp.where(ctx_first, time_previous_token[None, :], arrived), normed[:-1]], axis=0
    )
    inputs = [mixed_input(normed, previous, time_shift_weights[position]) for position in range(6)]
    recept = jnp.dot(inputs[0], receptance, preferred_element_type=F32).astype(BF16)
    keys = jnp.dot(inputs[2], key_projection_matrix, preferred_element_type=F32).astype(BF16)
    values = jnp.dot(inputs[3], value_projection_matrix, preferred_element_type=F32).astype(BF16)
    decay_low = jnp.tanh(
        jnp.dot(inputs[1], decay_first_factor, preferred_element_type=F32)
    ).astype(BF16)
    rate_low = jnp.dot(inputs[4], rate_first_factor, preferred_element_type=F32).astype(BF16)
    gate_low = jax.nn.sigmoid(
        jnp.dot(inputs[5], gate_first_factor, preferred_element_type=F32)
    ).astype(BF16)
    vec = jnp.stack(
        [
            decay_channel_base,
            rate_channel_base,
            removal_key_scale,
            key_rate_scale,
            self_lookup_coefficient,
            head_group_gain,
            head_group_bias,
            head_group_bias,
        ]
    )
    zero, reader, extra, moved = wkv_local(
        recept, keys, values, decay_low, rate_low, decay_second_factor, rate_second_factor, vec
    )
    arrivals = [passed_along(moved, "ctx", by) for by in range(1, lax.axis_size("ctx"))]
    lagged_embedding = wkv_finish(
        ctx_place.reshape(1).astype(jnp.int32),
        zero,
        reader,
        extra,
        gate_low,
        gate_second_factor,
        vec,
        head_state_initial,
        arrivals,
    )
    normed_next, middle = summed(
        "norm", 0, lagged_embedding, time_output_weight, own_rows(stream),
        channel_norm_gain, channel_norm_bias,
    )
    arrived_next = passed_along(normed_next[-1:], "ctx", 1)
    previous_next = jnp.concatenate(
        [jnp.where(ctx_first, channel_previous_token[None, :], arrived_next), normed_next[:-1]],
        axis=0,
    )
    channel_in = mixed_input(normed_next, previous_next, channel_shift_weight)
    expanded = jnp.maximum(
        jnp.dot(channel_in, channel_key_weight, preferred_element_type=jnp.float32), 0.0
    )
    hidden = (expanded * expanded).astype(jnp.bfloat16)
    layer_out, _ = summed(
        "plain", 1, hidden, channel_value_weight, middle, channel_norm_gain, channel_norm_bias
    )
    return layer_out


def solution(mesh):
    placed = (
        P("ctx", None),
        P(),
        P(),
        P("tp", None, None),
        P(),
        P(),
        P(),
        P(None, "tp"),
        P(None, "tp"),
        P(None, "tp"),
        P(),
        P(None, "tp"),
        P("tp"),
        P(),
        P(None, "tp"),
        P("tp"),
        P(),
        P(None, "tp"),
        P("tp"),
        P("tp"),
        P("tp"),
        P("tp"),
        P("tp"),
        P("tp", None),
        P(),
        P(),
        P(),
        P(None, "tp"),
        P("tp", None),
    )
    return jax.shard_map(
        shards, mesh=mesh, in_specs=placed, out_specs=P("ctx", None), check_vma=False
    )
```

```python
import functools

import jax
import jax.numpy as jnp
from jax import lax
from jax.experimental import pallas as pl
from jax.experimental.pallas import tpu as pltpu
from jax.sharding import PartitionSpec as P

LANE_SPAN = 64
SPAN = 64
PAIR = 2 * LANE_SPAN
F32 = jnp.float32
BF16 = jnp.bfloat16


def passed_along(shard, axis, by):
    length = lax.axis_size(axis)
    pairs = [(i, i + by) for i in range(length) if 0 <= i + by < length]
    return lax.ppermute(shard, axis, pairs)


def layer_norm(matrix, gain_vec, bias_vec):
    floats = matrix.astype(jnp.float32)
    average = jnp.mean(floats, axis=-1, keepdims=True)
    centered = floats - average
    variance = jnp.mean(centered * centered, axis=-1, keepdims=True)
    return (centered * lax.rsqrt(variance + 1e-05) * gain_vec + bias_vec).astype(jnp.bfloat16)


def mixed_input(normed, previous, weight_vec):
    current = normed.astype(jnp.float32)
    return (
        current + (previous.astype(jnp.float32) - current) * weight_vec.astype(jnp.float32)
    ).astype(jnp.bfloat16)


def mm(left, right):
    return jnp.dot(left.astype(BF16), right.astype(BF16), preferred_element_type=F32)


def mm_rt(left, right):
    return lax.dot_general(
        left.astype(BF16),
        right.astype(BF16),
        (((1,), (1,)), ((), ())),
        preferred_element_type=F32,
    )


def mm_lt(left, right):
    return lax.dot_general(
        left.astype(BF16),
        right.astype(BF16),
        (((0,), (0,)), ((), ())),
        preferred_element_type=F32,
    )


def split2(matrix):
    high = matrix.astype(BF16)
    return high, (matrix - high.astype(F32)).astype(BF16)


def head_ones():
    row = lax.broadcasted_iota(jnp.int32, (PAIR, PAIR), 0)
    col = lax.broadcasted_iota(jnp.int32, (PAIR, PAIR), 1)
    return ((row < LANE_SPAN) == (col < LANE_SPAN)).astype(BF16)


def head_sum(matrix, ones):
    high, low = split2(matrix)
    return jnp.dot(high, ones, preferred_element_type=F32) + jnp.dot(
        low, ones, preferred_element_type=F32
    )


def widened(matrix, same):
    return jnp.where(same, jnp.concatenate([matrix, matrix], axis=0), 0.0)


def folded(matrix):
    return matrix[:LANE_SPAN] + matrix[LANE_SPAN:]


def local_kernel(
    recept_ref, key_ref, value_ref, dlow_ref, rlow_ref, dsec_ref, rsec_ref, vec_ref,
    zero_ref, reader_ref, extra_ref, moved_ref,
    alpha_s, beta_s, logd_s, kadj_s,
):
    spans = recept_ref.shape[0] // SPAN
    ones = head_ones()
    vec = vec_ref[...]
    decay_raw = vec[0:1] + jnp.dot(dlow_ref[...], dsec_ref[...], preferred_element_type=F32)
    soft = jnp.maximum(-decay_raw, 0.0) + jnp.log1p(jnp.exp(-jnp.abs(decay_raw)))
    logd_s[...] = -jnp.exp(-soft - 0.5)
    rate = jax.nn.sigmoid(
        vec[1:2] + jnp.dot(rlow_ref[...], rsec_ref[...], preferred_element_type=F32)
    )
    keys = key_ref[...].astype(F32)
    scaled = keys * vec[2:3]
    norm_key = scaled * lax.rsqrt(head_sum(scaled * scaled, ones) + 1e-06)
    key_adj = keys * (1.0 + (rate - 1.0) * vec[3:4])
    recept_all = recept_ref[...].astype(F32)
    extra_ref[...] = (
        head_sum(recept_all * key_adj * vec[4:5], ones) * value_ref[...].astype(F32)
    )
    alpha_s[...] = -norm_key
    beta_s[...] = rate * norm_key
    kadj_s[...] = key_adj

    row = lax.broadcasted_iota(jnp.int32, (PAIR, PAIR), 0)
    col = lax.broadcasted_iota(jnp.int32, (PAIR, PAIR), 1)
    same = (row < LANE_SPAN) == (col < LANE_SPAN)
    strict = same & (row > col)
    inclusive = same & (row >= col)
    eye = (row == col).astype(F32)
    small_row = lax.broadcasted_iota(jnp.int32, (SPAN, SPAN), 0)
    small_col = lax.broadcasted_iota(jnp.int32, (SPAN, SPAN), 1)
    lower = (small_row >= small_col).astype(BF16)

    def levels():
        size = 1
        while size < SPAN:
            yield size, (row // (2 * size) == col // (2 * size)) & (row // size > col // size)
            size *= 2

    cuts = list(levels())

    stage = []
    for number in range(spans):
        at = pl.ds(number * SPAN, SPAN)
        logd = logd_s[at, :]
        high, low = split2(logd)
        cumulative = jnp.dot(lower, high, preferred_element_type=F32) + jnp.dot(
            lower, low, preferred_element_type=F32
        )
        before = cumulative - logd
        total = cumulative[SPAN - 1 : SPAN, :]
        centre = 0.5 * total
        grow = jnp.exp(centre - cumulative)
        half = jnp.exp(centre)
        left = alpha_s[at, :] * jnp.exp(before - centre)
        read = recept_ref[at, :].astype(F32) * jnp.exp(cumulative - centre)
        b_side = beta_s[at, :] * grow
        k_side = kadj_s[at, :] * grow
        wide_b = widened(b_side, same).astype(BF16)
        wide_k = widened(k_side, same).astype(BF16)
        wide_l = widened(left, same).astype(BF16)
        wide_r = widened(read, same).astype(BF16)
        pairs = mm_rt(
            jnp.concatenate([wide_l, wide_r], axis=0), jnp.concatenate([wide_b, wide_k], axis=0)
        )
        system = jnp.where(strict, pairs[:PAIR, :PAIR], 0.0)
        both = jnp.concatenate(
            [
                jnp.where(strict, pairs[:PAIR, PAIR:], 0.0),
                jnp.where(inclusive, pairs[PAIR:, PAIR:], 0.0),
            ],
            axis=0,
        ).astype(BF16)
        read_rate = jnp.where(inclusive, pairs[PAIR:, :PAIR], 0.0).astype(BF16)
        stage.append(
            dict(
                at=at, half=half, total=total, system=system.astype(BF16), both=both,
                read_rate=read_rate, left=left, read=read, b_side=b_side, k_side=k_side,
                inverse=eye + jnp.where(cuts[0][1], system, 0.0),
            )
        )
    for item in stage:
        item["wide_v"] = widened(value_ref[item["at"], :].astype(F32), same).astype(BF16)
        item["values"] = mm(item["both"], item["wide_v"])
    zero16 = jnp.zeros((PAIR, PAIR), BF16)
    for size, mask in cuts[1:]:
        for item in stage:
            item["inv16"] = item["inverse"].astype(BF16)
            item["step"] = mm(item["inv16"], jnp.where(mask, item["system"], zero16)).astype(BF16)
        for item in stage:
            item["inverse"] = item["inverse"] + mm(item["step"], item["inv16"])
    for item in stage:
        right_hand = jnp.concatenate(
            [item["values"][:PAIR], widened(item["left"] * item["half"], same)], axis=1
        )
        item["solved"] = mm(item["inverse"], right_hand).astype(BF16)
    chunks = []
    for item in stage:
        half = item["half"]
        seen = mm(item["read_rate"], item["solved"])
        zero = item["values"][PAIR:] + seen[:, :PAIR]
        reader = (widened(item["read"] * half, same) + seen[:, PAIR:]).astype(BF16)
        wide_be = widened(item["b_side"] * half, same).astype(BF16)
        wide_ke = widened(item["k_side"] * half, same).astype(BF16)
        moved = mm_lt(item["solved"], wide_be)
        update = moved[:PAIR] + mm_lt(item["wide_v"], wide_ke)
        chunks.append((zero, reader, moved[PAIR:].astype(BF16), update, jnp.exp(item["total"])))

    carry = jnp.concatenate([eye, jnp.zeros((PAIR, PAIR), F32)], axis=0)
    for number, (zero, reader, change, update, fade) in enumerate(chunks):
        at = pl.ds(number * SPAN, SPAN)
        carry16 = carry.astype(BF16)
        out = mm_rt(reader, carry16)
        reader_ref[at, :] = folded(out[:, :PAIR]).astype(BF16)
        zero_ref[at, :] = folded(zero + out[:, PAIR:])
        carry = carry * fade + jnp.dot(carry16, change, preferred_element_type=F32)
        carry = jnp.concatenate([carry[:PAIR], carry[PAIR:] + update], axis=0)
    moved_ref[0, 0] = folded(carry[:PAIR]).astype(BF16)
    moved_ref[0, 1] = folded(carry[PAIR:]).astype(BF16)


def wkv_local(half, recept, keys, values, dlow, rlow, dsec, rsec, vec):
    tokens = recept.shape[0]
    count = recept.shape[1] // PAIR // 2
    width = count * PAIR
    base = half * count
    by_pair = pl.BlockSpec((tokens, PAIR), lambda p: (0, p))
    picked = pl.BlockSpec((tokens, PAIR), lambda p: (0, p + base))
    whole = lambda a: pl.BlockSpec(a.shape, lambda p: (0, 0))
    cols = lambda a: pl.BlockSpec((a.shape[0], PAIR), lambda p: (0, p + base))
    return pl.pallas_call(
        local_kernel,
        grid=(count,),
        in_specs=[picked, picked, picked, whole(dlow), whole(rlow), cols(dsec), cols(rsec), cols(vec)],
        out_specs=[
            by_pair,
            by_pair,
            by_pair,
            pl.BlockSpec((1, 2, LANE_SPAN, PAIR), lambda p: (p, 0, 0, 0)),
        ],
        out_shape=[
            jax.ShapeDtypeStruct((tokens, width), F32),
            jax.ShapeDtypeStruct((tokens, width), BF16),
            jax.ShapeDtypeStruct((tokens, width), F32),
            jax.ShapeDtypeStruct((count, 2, LANE_SPAN, PAIR), BF16),
        ],
        scratch_shapes=[pltpu.VMEM((tokens, PAIR), F32)] * 4,
        compiler_params=pltpu.CompilerParams(vmem_limit_bytes=48 * 1024 * 1024),
        cost_estimate=pl.CostEstimate(
            flops=tokens * width * 4096, bytes_accessed=tokens * width * 20, transcendentals=tokens * width * 8
        ),
        name="wkv_local",
    )(recept, keys, values, dlow, rlow, dsec, rsec, vec)


def finish_kernel(place_ref, zero_ref, reader_ref, extra_ref, glow_ref, gsec_ref, vec_ref, state_ref, *rest):
    moved_refs, out_ref = rest[:-1], rest[-1]
    ones = head_ones()
    row = lax.broadcasted_iota(jnp.int32, (PAIR, PAIR), 0)
    col = lax.broadcasted_iota(jnp.int32, (PAIR, PAIR), 1)
    same = (row < LANE_SPAN) == (col < LANE_SPAN)
    state = jnp.concatenate([state_ref[0], state_ref[1]], axis=1)
    place = place_ref[0]
    for back in range(len(moved_refs), 0, -1):
        moved = moved_refs[back - 1]
        wide = widened(moved[0, 0].astype(F32), same).astype(BF16)
        high, low = split2(state)
        after = (
            jnp.dot(high, wide, preferred_element_type=F32)
            + jnp.dot(low, wide, preferred_element_type=F32)
            + moved[0, 1].astype(F32)
        )
        state = jnp.where(place >= back, after, state)
    wkv = zero_ref[...] + mm_rt(reader_ref[...], widened(state, same))
    scale = 1.0 / LANE_SPAN
    centered = wkv - head_sum(wkv, ones) * scale
    variance = head_sum(centered * centered, ones) * scale
    vec = vec_ref[...]
    normal = centered * lax.rsqrt(variance + 0.00064) * vec[5:6] + vec[6:7]
    gate = jnp.dot(glow_ref[...], gsec_ref[...], preferred_element_type=F32)
    out_ref[...] = ((normal + extra_ref[...]) * gate).astype(BF16)


def wkv_finish(half, place, zero, reader, extra, glow, gsec, vec, state, moved):
    tokens, width = zero.shape
    count = width // PAIR
    base = half * count
    by_pair = pl.BlockSpec((tokens, PAIR), lambda p: (0, p))
    whole = lambda a: pl.BlockSpec(a.shape, lambda p: (0, 0))
    cols = lambda a: pl.BlockSpec((a.shape[0], PAIR), lambda p: (0, p + base))
    return pl.pallas_call(
        finish_kernel,
        grid=(count,),
        in_specs=[
            pl.BlockSpec(memory_space=pltpu.SMEM),
            by_pair,
            by_pair,
            by_pair,
            whole(glow),
            cols(gsec),
            cols(vec),
            pl.BlockSpec((2, LANE_SPAN, LANE_SPAN), lambda p: (p + base, 0, 0)),
        ]
        + [pl.BlockSpec((1, 2, LANE_SPAN, PAIR), lambda p: (p, 0, 0, 0))] * len(moved),
        out_specs=by_pair,
        out_shape=jax.ShapeDtypeStruct((tokens, width), BF16),
        compiler_params=pltpu.CompilerParams(vmem_limit_bytes=48 * 1024 * 1024),
        cost_estimate=pl.CostEstimate(
            flops=tokens * width * 1024, bytes_accessed=tokens * width * 14, transcendentals=tokens * width
        ),
        name="wkv_finish",
    )(place, zero, reader, extra, glow, gsec, vec, state, *moved)


MESH = pl.DeviceIdType.MESH


def summed_kernel(
    way, places, count, *refs
):
    left_refs = refs[:count]
    (
        right_ref, rest_ref, gain_ref, bias_ref, out_ref, kept_ref, last_ref,
        part_ref, acc_ref, recv_ref, rs_send, rs_recv, ag_send, ag_recv, row_sem,
    ) = refs[count:]
    bits = places.bit_length() - 1
    tokens, width = out_ref.shape
    rows = tokens // places
    parts = acc_ref.shape[0]
    wide = width // parts
    me = lax.axis_index("tp")
    mine = [(me // (1 << d)) % 2 for d in range(bits)]
    partners = [me + (1 << d) * (1 - 2 * mine[d]) for d in range(bits)]
    orders = [list(range(bits)), list(range(1)) + list(range(bits - 1, 0, -1))] * (parts // 2)
    weight = [1 << (bits - 1 - d) for d in range(bits)]

    def frees(order, step):
        dims = order[step + 1 :]
        for code in range(1 << len(dims)):
            yield code, {d: (code >> n) % 2 for n, d in enumerate(dims)}

    def block(free, flipped=None):
        total = 0
        for d in range(bits):
            value = free[d] if d in free else (1 - mine[d] if d == flipped else mine[d])
            total = total + value * weight[d]
        return total

    def area(at, side):
        return pl.ds(pl.multiple_of(at * rows, rows), rows), pl.ds(side * wide, wide)

    barrier = pltpu.get_barrier_semaphore()
    for partner in partners:
        pl.semaphore_signal(barrier, inc=1, device_id={"tp": partner}, device_id_type=MESH)
    if way == "norm":
        blocks = lax.axis_size("ctx")
        place = lax.axis_index("ctx")
        after = lax.rem(place + 1, blocks)
        for other in (after, lax.rem(place + blocks - 1, blocks)):
            pl.semaphore_signal(barrier, inc=1, device_id={"ctx": other}, device_id_type=MESH)
        pl.semaphore_wait(barrier, bits + 2)
    else:
        pl.semaphore_wait(barrier, bits)

    def product(first, side):
        group = pl.ds(pl.multiple_of(first * (tokens // 2), tokens // 2), tokens // 2)
        tile = 512

        def one(tile_number, _):
            cols = pl.ds(pl.multiple_of(side * wide + tile_number * tile, tile), tile)
            depth = right_ref.shape[0] // count
            part_ref[group, cols] = sum(
                jnp.dot(
                    left_refs[n][group, :],
                    right_ref[n * depth : (n + 1) * depth, cols],
                    preferred_element_type=F32,
                )
                for n in range(count)
            ).astype(BF16)
            return 0

        lax.fori_loop(0, wide // tile, one, 0)

    starts = [places - (1 << (bits - step)) for step in range(bits)]
    sent = []

    def scatter(side, step, code, free):
        order = orders[side]
        dim = order[step]
        slot = starts[step] + code
        at = block(free, dim)
        source = part_ref.at[area(at, side)] if step == 0 else acc_ref.at[side, at]
        copy = pltpu.make_async_remote_copy(
            src_ref=source,
            dst_ref=recv_ref.at[side, slot],
            send_sem=rs_send.at[side, slot],
            recv_sem=rs_recv.at[side, slot],
            device_id={"tp": partners[dim]},
            device_id_type=MESH,
        )
        copy.start()
        sent.append(copy)

    def gathered(side, step, code, free):
        order = orders[side]
        slot = starts[step] + code
        at = block(free)
        pltpu.make_async_remote_copy(
            src_ref=recv_ref.at[side, slot],
            dst_ref=recv_ref.at[side, slot],
            send_sem=rs_send.at[side, slot],
            recv_sem=rs_recv.at[side, slot],
            device_id={"tp": partners[order[step]]},
            device_id_type=MESH,
        ).wait_recv()
        base = pl.multiple_of(at * rows, rows)
        tile = 16

        def one(n, _):
            here = pl.ds(pl.multiple_of(n * tile, tile), tile)
            if step == 0:
                there = pl.ds(pl.multiple_of(base + n * tile, tile), tile)
                own = part_ref[there, pl.ds(side * wide, wide)]
            else:
                own = acc_ref[side, at, here, :]
            acc_ref[side, at, here, :] = (
                own.astype(F32) + recv_ref[side, slot, here, :].astype(F32)
            ).astype(BF16)
            return 0

        lax.fori_loop(0, rows // tile, one, 0)

    for side in range(parts):
        product(1 - mine[0], side)
        for code, free in frees(orders[side], 0):
            scatter(side, 0, code, free)
    for step in range(bits):
        for side in range(parts):
            if step == 0:
                product(mine[0], side)
            for code, free in frees(orders[side], step):
                gathered(side, step, code, free)
            if step + 1 < bits:
                for code, free in frees(orders[side], step + 1):
                    scatter(side, step + 1, code, free)

    here_block = block({})
    base = pl.multiple_of(here_block * rows, rows)
    tile = 16

    def finish(n, _):
        here = pl.ds(pl.multiple_of(n * tile, tile), tile)
        there = pl.ds(pl.multiple_of(base + n * tile, tile), tile)
        total = jnp.concatenate(
            [acc_ref[side, here_block, here, :] for side in range(parts)], axis=1
        ).astype(F32)
        middle = (rest_ref[here, :].astype(F32) + total).astype(BF16)
        if way == "norm":
            kept_ref[here, :] = middle
            floats = middle.astype(F32)
            centered = floats - jnp.mean(floats, axis=-1, keepdims=True)
            variance = jnp.mean(centered * centered, axis=-1, keepdims=True)
            middle = (
                centered * lax.rsqrt(variance + 1e-05) * gain_ref[...] + bias_ref[...]
            ).astype(BF16)
        out_ref[there, :] = middle
        return 0

    lax.fori_loop(0, rows // tile, finish, 0)
    if way != "norm":
        kept_ref[...] = jnp.zeros_like(kept_ref)
        last_ref[...] = jnp.zeros_like(last_ref)

    def share(side, step, at):
        dim = orders[side][step]
        copy = pltpu.make_async_remote_copy(
            src_ref=out_ref.at[area(at, side)],
            dst_ref=out_ref.at[area(at, side)],
            send_sem=ag_send.at[side, step, at],
            recv_sem=ag_recv.at[side, at],
            device_id={"tp": partners[dim]},
            device_id_type=MESH,
        )
        copy.start()
        sent.append(copy)

    for step in range(bits - 1, -1, -1):
        for side in range(parts):
            share(side, step, here_block)
    for step in range(bits - 1, -1, -1):
        for side in range(parts):
            for code, free in frees(orders[side], step):
                at = block(free, orders[side][step])
                pltpu.make_async_remote_copy(
                    src_ref=out_ref.at[area(at, side)],
                    dst_ref=out_ref.at[area(at, side)],
                    send_sem=ag_send.at[side, step, at],
                    recv_sem=ag_recv.at[side, at],
                    device_id={"tp": partners[orders[side][step]]},
                    device_id_type=MESH,
                ).wait_recv()
                for later in range(step - 1, -1, -1):
                    share(side, later, at)
    if way == "norm":
        copy = pltpu.make_async_remote_copy(
            src_ref=out_ref.at[pl.ds(tokens - 16, 16), :],
            dst_ref=last_ref,
            send_sem=row_sem.at[0],
            recv_sem=row_sem.at[1],
            device_id={"ctx": after},
            device_id_type=MESH,
        )
        copy.start()
        copy.wait_recv()
        sent.append(copy)
    for copy in sent:
        copy.wait_send()


def summed(way, number, left, right, rest, gain, bias):
    parts = 4
    places = lax.axis_size("tp")
    bits = places.bit_length() - 1
    tokens = rest.shape[0] * places
    width = right.shape[1]
    rows = tokens // places
    small = (rows, width) if way == "norm" else (8, 128)
    vmem = pl.BlockSpec(memory_space=pltpu.VMEM)
    left_specs = [vmem] * len(left)
    lefts = left
    return pl.pallas_call(
        functools.partial(summed_kernel, way, places, len(left)),
        in_specs=left_specs + [vmem] * 4,
        out_specs=[vmem, vmem, vmem],
        out_shape=[
            jax.ShapeDtypeStruct((tokens, width), BF16),
            jax.ShapeDtypeStruct(small, BF16),
            jax.ShapeDtypeStruct((16, width) if way == "norm" else (16, 128), BF16),
        ],
        scratch_shapes=[
            pltpu.VMEM((tokens, width), BF16),
            pltpu.VMEM((parts, places, rows, width // parts), BF16),
            pltpu.VMEM((parts, places - 1, rows, width // parts), BF16),
            pltpu.SemaphoreType.DMA((parts, places - 1)),
            pltpu.SemaphoreType.DMA((parts, places - 1)),
            pltpu.SemaphoreType.DMA((parts, bits, places)),
            pltpu.SemaphoreType.DMA((parts, places)),
            pltpu.SemaphoreType.DMA((2,)),
        ],
        compiler_params=pltpu.CompilerParams(
            collective_id=number, has_side_effects=True, vmem_limit_bytes=56 * 1024 * 1024
        ),
        name="summed_" + way,
    )(*lefts, right, rest, gain.reshape(1, -1), bias.reshape(1, -1))


def own_rows(matrix):
    places = lax.axis_size("tp")
    bits = places.bit_length() - 1
    me = lax.axis_index("tp")
    place = sum(((me // (1 << d)) % 2) * (1 << (bits - 1 - d)) for d in range(bits))
    rows = matrix.shape[0] // places
    return lax.dynamic_slice_in_dim(matrix, place * rows, rows, axis=0)


def shards(
    stream,
    time_previous_token,
    channel_previous_token,
    head_state_initial,
    time_norm_gain,
    time_norm_bias,
    time_shift_weights,
    receptance,
    key_projection_matrix,
    value_projection_matrix,
    decay_first_factor,
    decay_second_factor,
    decay_channel_base,
    rate_first_factor,
    rate_second_factor,
    rate_channel_base,
    gate_first_factor,
    gate_second_factor,
    removal_key_scale,
    key_rate_scale,
    self_lookup_coefficient,
    head_group_gain,
    head_group_bias,
    time_output_weight,
    channel_norm_gain,
    channel_norm_bias,
    channel_shift_weight,
    channel_key_weight,
    channel_value_weight,
):
    normed = layer_norm(stream, time_norm_gain, time_norm_bias)
    ctx_place = lax.axis_index("ctx")
    ctx_first = ctx_place == 0
    arrived = passed_along(
        layer_norm(lax.optimization_barrier(stream[-1:]), time_norm_gain, time_norm_bias), "ctx", 1
    )
    previous = jnp.concatenate(
        [jnp.where(ctx_first, time_previous_token[None, :], arrived), normed[:-1]], axis=0
    )
    inputs = [mixed_input(normed, previous, time_shift_weights[position]) for position in range(6)]
    recept = jnp.dot(inputs[0], receptance, preferred_element_type=F32).astype(BF16)
    keys = jnp.dot(inputs[2], key_projection_matrix, preferred_element_type=F32).astype(BF16)
    values = jnp.dot(inputs[3], value_projection_matrix, preferred_element_type=F32).astype(BF16)
    decay_low = jnp.tanh(
        jnp.dot(inputs[1], decay_first_factor, preferred_element_type=F32)
    ).astype(BF16)
    rate_low = jnp.dot(inputs[4], rate_first_factor, preferred_element_type=F32).astype(BF16)
    gate_low = jax.nn.sigmoid(
        jnp.dot(inputs[5], gate_first_factor, preferred_element_type=F32)
    ).astype(BF16)
    vec = jnp.stack(
        [
            decay_channel_base,
            rate_channel_base,
            removal_key_scale,
            key_rate_scale,
            self_lookup_coefficient,
            head_group_gain,
            head_group_bias,
            head_group_bias,
        ]
    )
    locals_ = [
        wkv_local(
            half, recept, keys, values, decay_low, rate_low,
            decay_second_factor, rate_second_factor, vec,
        )
        for half in range(2)
    ]
    arrivals = [
        [passed_along(parts[3], "ctx", by) for by in range(1, lax.axis_size("ctx"))]
        for parts in locals_
    ]
    lagged_embedding = [
        wkv_finish(
            half,
            ctx_place.reshape(1).astype(jnp.int32),
            *locals_[half][:3],
            gate_low,
            gate_second_factor,
            vec,
            head_state_initial,
            arrivals[half],
        )
        for half in range(2)
    ]
    normed_next, middle, last_rows = summed(
        "norm", 0, lagged_embedding, time_output_weight, own_rows(stream),
        channel_norm_gain, channel_norm_bias,
    )
    arrived_next = last_rows[-1:]
    previous_next = jnp.concatenate(
        [jnp.where(ctx_first, channel_previous_token[None, :], arrived_next), normed_next[:-1]],
        axis=0,
    )
    channel_in = mixed_input(normed_next, previous_next, channel_shift_weight)
    expanded = jnp.maximum(
        jnp.dot(channel_in, channel_key_weight, preferred_element_type=jnp.float32), 0.0
    )
    hidden = (expanded * expanded).astype(jnp.bfloat16)
    layer_out, _, _ = summed(
        "plain", 1, [hidden], channel_value_weight, middle, channel_norm_gain, channel_norm_bias
    )
    return layer_out


def solution(mesh):
    placed = (
        P("ctx", None),
        P(),
        P(),
        P("tp", None, None),
        P(),
        P(),
        P(),
        P(None, "tp"),
        P(None, "tp"),
        P(None, "tp"),
        P(),
        P(None, "tp"),
        P("tp"),
        P(),
        P(None, "tp"),
        P("tp"),
        P(),
        P(None, "tp"),
        P("tp"),
        P("tp"),
        P("tp"),
        P("tp"),
        P("tp"),
        P("tp", None),
        P(),
        P(),
        P(),
        P(None, "tp"),
        P("tp", None),
    )
    return jax.shard_map(
        shards, mesh=mesh, in_specs=placed, out_specs=P("ctx", None), check_vma=False
    )
```
